32 devices in a mesh: dp: 8 (over z, y), tensor: 4 (over x, core).
Axes of the slice: x: 2, y: 2, z: 4, core: 2. Of those that a mesh axis runs over, the one named last changes fastest.
Arguments:
- tokens: bfloat16 [16384, 2048], P(('dp', 'tensor')), may hold values from -6 to 6
- attn_gain: bfloat16 [2048], P('dp'), may hold values from 0.099609375 to 1.8984375
- w_query: bfloat16 [2048, 1024], P('dp', 'tensor'), may hold values from -0.125 to 0.125
- key_matrix: bfloat16 [2048, 256], P('dp', 'tensor'), may hold values from -0.125 to 0.125
- value_matrix: bfloat16 [2048, 256], P('dp', 'tensor'), may hold values from -0.125 to 0.125
- query_gain: bfloat16 [64], replicated, may hold values from 0.099609375 to 1.8984375
- key_gain: bfloat16 [64], replicated, may hold values from 0.099609375 to 1.8984375
- w_out: bfloat16 [1024, 2048], P('tensor', 'dp'), may hold values from -0.75 to 0.75
- ffn_gain: bfloat16 [2048], P('dp'), may hold values from 0.099609375 to 1.8984375
- w_gate: bfloat16 [2048, 1792], P('dp', 'tensor'), may hold values from -0.125 to 0.125
- w_up: bfloat16 [2048, 1792], P('dp', 'tensor'), may hold values from -0.125 to 0.125
- w_down: bfloat16 [1792, 2048], P('tensor', 'dp'), may hold values from -0.125 to 0.125
- out_grad: bfloat16 [16384, 2048], P(('dp', 'tensor')), may hold values from -6 to 6
- seq_lengths: int32 [16], replicated, may hold values from 1024 to 1024, as said below
- seq_order: int32 [16], replicated, may hold values from 0 to 15, as said below
Outputs:
- layer_out: bfloat16 [16384, 2048], P(('dp', 'tensor'))
- input_grad: bfloat16 [16384, 2048], P(('dp', 'tensor'))
- grad_attn_gain: float32 [2048], P('dp')
- grad_w_query: float32 [2048, 1024], P('dp', 'tensor')
- grad_w_key: float32 [2048, 256], P('dp', 'tensor')
- grad_w_value: float32 [2048, 256], P('dp', 'tensor')
- grad_query_gain: float32 [64], replicated
- grad_key_gain: float32 [64], replicated
- grad_w_out: float32 [1024, 2048], P('tensor', 'dp')
- grad_ffn_gain: float32 [2048], P('dp')
- grad_w_gate: float32 [2048, 1792], P('dp', 'tensor')
- grad_w_up: float32 [2048, 1792], P('dp', 'tensor')
- grad_w_down: float32 [1792, 2048], P('tensor', 'dp')
The draws below stay inside these ranges and needn't reach their ends.
Inputs may be any that keep to these rules, and one draw needn't show every extreme that they name: seq_order holds every sequence number once. `seq_lengths`: the two sequences of each group together have 2048 tokens.
All inputs are finite; a program needn't handle non-finite values.
Results may differ from the reference program's by a relative error of at most 0.018.
Values may be sent and summed in bfloat16 or wider, within the bound.
No kernel may reach another device: no remote copies, remote signals or barrier semaphores. Data moves between devices by JAX's collectives and lax.ppermute only.
A program may use at most 256 MiB of HBM per device.

```python
from functools import partial
import jax
import jax.numpy as jnp
from jax import lax

MODEL_WIDTH = 2048
QUERY_HEADS = 16
KEY_VALUE_HEADS = 4
HEAD_WIDTH = 64
FF = 1792
MIN_LEN = 1024
GROUP_TOK = 2048
TOKENS = 16384
NSEQ = 16


def paired_slots(key):
    groups = NSEQ // 2
    base = jax.random.fold_in(key, 11)
    order = jax.random.permutation(jax.random.fold_in(base, 1), NSEQ).astype(jnp.int32)
    firsts = jax.random.randint(jax.random.fold_in(base, 2), (groups,), MIN_LEN, GROUP_TOK - MIN_LEN + 1, dtype=jnp.int32)
    pinned = jax.random.randint(jax.random.fold_in(base, 3), (), 0, groups, dtype=jnp.int32)
    firsts = jnp.where(jnp.arange(groups, dtype=jnp.int32) == pinned, MIN_LEN, firsts).astype(jnp.int32)
    slot_lengths = jnp.stack([firsts, GROUP_TOK - firsts], axis=1).reshape(NSEQ).astype(jnp.int32)
    lengths = jnp.zeros((NSEQ,), jnp.int32).at[order].set(slot_lengths)
    return (lengths, order)


def draw_seq_lengths(key, part):
    return paired_slots(key)[0]


def draw_seq_order(key, part):
    return paired_slots(key)[1]


def with_spikes(values, key, source, target, parts, factor):
    def block_of(dim):
        return (jnp.arange(values.shape[dim]) // (values.shape[dim] // parts)).reshape((-1,) + (1,) * (values.ndim - 1 - dim))

    near = jax.random.permutation(key, parts)[block_of(target)]
    other_side = (block_of(target) + parts // 2) % parts
    return jnp.where((block_of(source) == near) | (block_of(source) == other_side), factor * values, values)


def block_scale(rng, shape, pieces, low, largest):
    level = 1.0
    for axis_at, parts in pieces:
        draws = jax.random.uniform(jax.random.fold_in(jax.random.fold_in(rng, 6), axis_at), (parts,), jnp.float32, low / len(pieces), largest / len(pieces))
        level = level * jnp.repeat(jnp.exp(draws), shape[axis_at] // parts).reshape((-1,) + (1,) * (len(shape) - 1 - axis_at))
    return level


def noise(key, shape, width, reach, cuts=(), kind=jnp.bfloat16):
    values = jax.random.normal(key, shape, jnp.float32) * width
    if len(cuts) > 0:
        values = block_scale(key, shape, cuts, -0.22, 0.18) * values
    return jnp.clip(values, min=-reach, max=reach).astype(kind)


def bell_draw_with(rng, dims, spread, bound, cuts, heavy, kind=jnp.bfloat16):
    array = spread * jax.random.normal(rng, dims, jnp.float32)
    if cuts:
        array = array * block_scale(rng, dims, cuts, -0.22, 0.18)
    return jnp.clip(with_spikes(array, jax.random.fold_in(rng, 3), *heavy), -bound, bound).astype(kind)


def setup_inputs(seed: int = 0) -> dict:
    key_list = jax.random.split(jax.random.key(seed), 16)
    return {
        "tokens": bell_draw_with(key_list[0], (TOKENS, MODEL_WIDTH), 1.0, 6.0, ((0, 32),), (0, 1, 32, 2.75)),
        "attn_gain": jnp.clip(1.0 + 0.18 * jax.random.normal(key_list[1], (MODEL_WIDTH,), jnp.float32), 0.099609375, 1.8984375).astype(jnp.bfloat16),
        "w_query": noise(key_list[2], (MODEL_WIDTH, QUERY_HEADS * HEAD_WIDTH), MODEL_WIDTH ** -0.5, 0.125, ((0, 8), (1, 4))),
        "key_matrix": noise(key_list[3], (MODEL_WIDTH, KEY_VALUE_HEADS * HEAD_WIDTH), MODEL_WIDTH ** -0.5, 0.125, ((0, 8), (1, 4))),
        "value_matrix": noise(key_list[4], (MODEL_WIDTH, KEY_VALUE_HEADS * HEAD_WIDTH), MODEL_WIDTH ** -0.5, 0.125, ((0, 8), (1, 4))),
        "query_gain": jnp.clip(1.0 + 0.18 * jax.random.normal(key_list[5], (HEAD_WIDTH,), jnp.float32), 0.099609375, 1.8984375).astype(jnp.bfloat16),
        "key_gain": jnp.clip(1.0 + 0.18 * jax.random.normal(key_list[6], (HEAD_WIDTH,), jnp.float32), 0.099609375, 1.8984375).astype(jnp.bfloat16),
        "w_out": noise(key_list[7], (QUERY_HEADS * HEAD_WIDTH, MODEL_WIDTH), (QUERY_HEADS * HEAD_WIDTH // 16) ** -0.5, 0.75, ((0, 4), (1, 8))),
        "ffn_gain": jnp.clip(1.0 + 0.18 * jax.random.normal(key_list[8], (MODEL_WIDTH,), jnp.float32), 0.099609375, 1.8984375).astype(jnp.bfloat16),
        "w_gate": noise(key_list[9], (MODEL_WIDTH, FF), MODEL_WIDTH ** -0.5, 0.125, ((0, 8), (1, 4))),
        "w_up": noise(key_list[10], (MODEL_WIDTH, FF), MODEL_WIDTH ** -0.5, 0.125, ((0, 8), (1, 4))),
        "w_down": noise(key_list[11], (FF, MODEL_WIDTH), FF ** -0.5, 0.125, ((0, 4), (1, 8))),
        "out_grad": noise(key_list[12], (TOKENS, MODEL_WIDTH), 1.0, 6.0, ((0, 32),)),
        "seq_lengths": draw_seq_lengths(jax.random.fold_in(key_list[15], 71), 0),
        "seq_order": draw_seq_order(jax.random.fold_in(key_list[15], 71), 0),
    }


@jax.custom_vjp
def low(v):
    return lax.optimization_barrier(v.astype(jnp.bfloat16)).astype(jnp.float32)

@jax.custom_vjp
def reduced_backward(v):
    return v

def low_keep(v):
    return (low(v), None)

def low_pass(kept, grad):
    return (grad,)

def back_keep(v):
    return (v, None)

def back_low(kept, grad):
    return (low(grad),)
low.defvjp(low_keep, low_pass)
reduced_backward.defvjp(back_keep, back_low)
EPS = 1e-06
THETA = 10000.0
HIGHEST = lax.Precision.HIGHEST

def matrix_product(left, right):
    return jnp.dot(left, right, precision=HIGHEST, preferred_element_type=jnp.float32)

def rms_norm(values, gain):
    return values * lax.rsqrt(lax.optimization_barrier(jnp.mean(values * values, axis=-1, keepdims=True)) + EPS) * gain

def rotate(values, position):
    half = values.shape[-1] // 2
    freqs = THETA ** (-(jnp.arange(half, dtype=jnp.float32) * 2.0 / values.shape[-1]))
    angles = position[:, None] * freqs[None, :]
    cosine = jnp.cos(angles)[:, None, :]
    sine = jnp.sin(angles)[:, None, :]
    first = values[..., :half]
    later = values[..., half:]
    return jnp.concatenate([first * cosine - later * sine, first * sine + later * cosine], axis=-1)

def forward(first_len, inputs, attn_gain, w_query, key_matrix, value_matrix, query_gain, key_gain, w_out, ffn_gain, w_gate, w_up, w_down):
    grouped_row_list = inputs.shape[0]
    row_ids = jnp.arange(grouped_row_list, dtype=jnp.int32)
    second = row_ids >= first_len
    position = (row_ids - jnp.where(second, first_len, 0)).astype(jnp.float32)
    normalized_attention = low(rms_norm(inputs, attn_gain))
    query = reduced_backward(matrix_product(normalized_attention, w_query)).reshape(grouped_row_list, QUERY_HEADS, HEAD_WIDTH)
    key = reduced_backward(matrix_product(normalized_attention, key_matrix)).reshape(grouped_row_list, KEY_VALUE_HEADS, HEAD_WIDTH)
    value_rows = reduced_backward(matrix_product(normalized_attention, value_matrix)).reshape(grouped_row_list, KEY_VALUE_HEADS, HEAD_WIDTH)
    query_rot = low(rotate(rms_norm(query, query_gain), position))
    key_rot = low(rotate(rms_norm(key, key_gain), position))
    value_low = low(value_rows)
    common_tensors = QUERY_HEADS // KEY_VALUE_HEADS
    key_wide = jnp.repeat(key_rot, common_tensors, axis=1)
    value_wide = jnp.repeat(value_low, common_tensors, axis=1)
    block = min(512, grouped_row_list)
    block_count = grouped_row_list // block

    def attend_block(block_data):
        query_block, rows_block = block_data
        scores = reduced_backward(jnp.einsum('qhd,khd->hqk', query_block, key_wide, precision=HIGHEST) * HEAD_WIDTH ** (-0.5))
        second_block = rows_block >= first_len
        allowed = (row_ids[None, :] <= rows_block[:, None]) & (second[None, :] == second_block[:, None])
        probs = jax.nn.softmax(jnp.where(allowed[None], scores, -1e+30), axis=-1)
        return jnp.einsum('hqk,khd->qhd', low(probs), value_wide, precision=HIGHEST)
    attention = lax.map(jax.checkpoint(attend_block), (query_rot.reshape(block_count, block, QUERY_HEADS, HEAD_WIDTH), row_ids.reshape(block_count, block)))
    attention = low(reduced_backward(attention.reshape(grouped_row_list, QUERY_HEADS, HEAD_WIDTH))).reshape(grouped_row_list, QUERY_HEADS * HEAD_WIDTH)
    hidden_res = inputs + reduced_backward(matrix_product(attention, w_out))
    normed_ffn = low(rms_norm(hidden_res, ffn_gain))
    gate = reduced_backward(matrix_product(normed_ffn, w_gate))
    upper = reduced_backward(matrix_product(normed_ffn, w_up))
    inner = low(jax.nn.silu(gate) * upper)
    return hidden_res + reduced_backward(matrix_product(inner, w_down))

def reference(tokens, attn_gain, w_query, key_matrix, value_matrix, query_gain, key_gain, w_out, ffn_gain, w_gate, w_up, w_down, out_grad, seq_lengths, seq_order):
    groups = seq_order.shape[0] // 2
    grouped_row_list = tokens.shape[0] // groups
    weights = tuple((weight.astype(jnp.float32) for weight in (attn_gain, w_query, key_matrix, value_matrix, query_gain, key_gain, w_out, ffn_gain, w_gate, w_up, w_down)))
    first_lens = jnp.take(seq_lengths, seq_order[0::2]).astype(jnp.int32)
    inputs = tokens.astype(jnp.float32).reshape(groups, grouped_row_list, MODEL_WIDTH)
    cotangents = out_grad.astype(jnp.float32).reshape(groups, grouped_row_list, MODEL_WIDTH)

    def one_group(running, group_data):
        first_len, group_in, group_cot = group_data
        result, pullback = jax.vjp(partial(forward, first_len), group_in, *weights)
        grads = pullback(group_cot)
        updated = tuple((total + grad for total, grad in zip(running, grads[1:])))
        return (updated, (result.astype(jnp.bfloat16), grads[0].astype(jnp.bfloat16)))
    zeros = tuple((jnp.zeros_like(weight) for weight in weights))
    totals, (results, in_grads) = lax.scan(one_group, zeros, (first_lens, inputs, cotangents))
    return (results.reshape(-1, MODEL_WIDTH), in_grads.reshape(-1, MODEL_WIDTH), totals[0], totals[1], totals[2], totals[3], totals[4], totals[5], totals[6], totals[7], totals[8], totals[9], totals[10])
```

```python
import jax
import jax.numpy as jnp
from jax import lax
from jax.sharding import PartitionSpec as P

EPS = 1e-06
THETA = 10000.0
F32 = jnp.float32
BF16 = jnp.bfloat16


def swap_core(a):
    return lax.ppermute(a, "tensor", [(t, t ^ 1) for t in range(lax.axis_size("tensor"))])


def swap_x(a):
    return lax.ppermute(a, "tensor", [(t, t ^ 2) for t in range(lax.axis_size("tensor"))])


def swap_dp(a, k):
    return lax.ppermute(a, "dp", [(d, d ^ k) for d in range(lax.axis_size("dp"))])


def gather(block, axis, by_x):
    half = lax.axis_size("dp") // 2
    q00 = jnp.concatenate([block] + [swap_dp(block, 2 * k) for k in range(1, half)], axis=axis)
    q01 = swap_dp(q00, 1)
    q10 = swap_x(q00)
    q11 = swap_x(q01) if by_x else swap_dp(q10, 1)
    return q00, q01, q10, q11


def add(*parts):
    total = parts[0].astype(F32)
    for part in parts[1:]:
        total = total + part.astype(F32)
    return total


def scatter(quarters, axis, by_x):
    q00, q01, q10, q11 = quarters
    half = lax.axis_size("dp") // 2
    if by_x:
        q01 = add(q01, swap_x(q11)).astype(BF16)
    else:
        q10 = add(q10, swap_dp(q11, 1)).astype(BF16)
    own = add(q00, swap_dp(q01, 1), swap_x(q10)).astype(BF16)
    blocks = jnp.split(own, half, axis=axis)
    return add(blocks[0], *[swap_dp(blocks[k], 2 * k) for k in range(1, half)])


def rotate(values, cosine, sine):
    half = values.shape[-1] // 2
    first = values[..., :half]
    later = values[..., half:]
    return jnp.concatenate([first * cosine - later * sine, first * sine + later * cosine], axis=-1)


def unrotate(values, cosine, sine):
    half = values.shape[-1] // 2
    first = values[..., :half]
    later = values[..., half:]
    return jnp.concatenate([first * cosine + later * sine, later * cosine - first * sine], axis=-1)


def norm_back(values, rms, gain, upstream):
    scaled = upstream * gain
    grad_values = rms * scaled - values * (rms * rms * rms) * jnp.mean(
        scaled * values, axis=-1, keepdims=True
    )
    grad_gain = jnp.sum(upstream * values * rms, axis=0)
    return (grad_values, grad_gain)


def dot(a, b, dims=((1,), (0,))):
    return lax.dot_general(a, b, (dims, ((), ())), preferred_element_type=F32)


def attend(query, key_raw, value_raw, gain_query, gain_key, cosine, sine, block):
    rows, heads, size = query.shape
    scale = size ** (-0.5)
    query_rms = lax.rsqrt(jnp.mean(query * query, axis=-1, keepdims=True) + EPS)
    query_rot = rotate(query * query_rms * gain_query, cosine[:, None], sine[:, None]).astype(BF16)
    key_rms = lax.rsqrt(jnp.mean(key_raw * key_raw, axis=-1, keepdims=True) + EPS)
    key_rot = rotate(key_raw * key_rms * gain_key, cosine, sine).astype(BF16)
    value_low = value_raw.astype(BF16)
    row_ids = jnp.arange(rows, dtype=jnp.int32)

    def masked_scores(start, stop):
        raw = jnp.einsum("qhd,kd->hqk", query_rot[start:stop], key_rot[:stop], preferred_element_type=F32) * scale
        allowed = row_ids[None, :stop] <= row_ids[start:stop, None]
        return (jnp.where(allowed[None], raw, -1e30), allowed)

    outs, lses = [], []
    for start in range(0, rows, block):
        stop = start + block
        masked, _ = masked_scores(start, stop)
        highest = jnp.max(masked, axis=-1, keepdims=True)
        expo = jnp.exp(masked - highest)
        total = jnp.sum(expo, axis=-1, keepdims=True)
        probs_low = (expo / total).astype(BF16)
        lses.append(highest + jnp.log(total))
        outs.append(jnp.einsum("hqk,kd->qhd", probs_low, value_low[:stop], preferred_element_type=F32))
    attention = jnp.concatenate(outs, axis=0).reshape(rows, heads * size).astype(BF16)

    def backward(d_attention):
        d_attention = d_attention.reshape(rows, heads, size)
        query_grads = []
        key_grad = jnp.zeros((rows, size), F32)
        value_grad = jnp.zeros((rows, size), F32)
        for index, start in enumerate(range(0, rows, block)):
            stop = start + block
            masked, allowed = masked_scores(start, stop)
            probs = jnp.where(allowed[None], jnp.exp(masked - lses[index]), 0.0)
            probs_low = probs.astype(BF16)
            d_block = d_attention[start:stop]
            d_probs = jnp.einsum("qhd,kd->hqk", d_block, value_low[:stop], preferred_element_type=F32)
            delta = jnp.sum(probs * d_probs, axis=-1, keepdims=True)
            d_scores = (probs * (d_probs - delta)).astype(BF16)
            query_grads.append(jnp.einsum("hqk,kd->qhd", d_scores, key_rot[:stop], preferred_element_type=F32) * scale)
            key_grad = key_grad.at[:stop].add(
                jnp.einsum("hqk,qhd->kd", d_scores, query_rot[start:stop], preferred_element_type=F32) * scale
            )
            value_grad = value_grad.at[:stop].add(
                jnp.einsum("hqk,qhd->kd", probs_low, d_block, preferred_element_type=F32)
            )
        query_norm_grad = unrotate(jnp.concatenate(query_grads, axis=0), cosine[:, None], sine[:, None])
        query_raw_grad, grad_query_gain = norm_back(
            query.reshape(-1, size), query_rms.reshape(-1, 1), gain_query, query_norm_grad.reshape(-1, size)
        )
        key_norm_grad = unrotate(key_grad, cosine, sine)
        key_raw_grad, grad_key_gain = norm_back(key_raw, key_rms, gain_key, key_norm_grad)
        grad = jnp.concatenate(
            [query_raw_grad.reshape(rows, heads * size), key_raw_grad, value_grad], axis=1
        ).astype(BF16)
        return grad, grad_query_gain, grad_key_gain

    return attention, backward


def body(
    tokens,
    attn_gain,
    w_query,
    key_matrix,
    value_matrix,
    query_gain,
    key_gain,
    w_out,
    ffn_gain,
    w_gate,
    w_up,
    w_down,
    out_grad,
    seq_lengths,
    seq_order,
):
    rows, width = tokens.shape
    chip_rows = 2 * rows
    head_size = query_gain.shape[0]
    query_width = w_query.shape[1]
    head_count = query_width // head_size
    units = w_gate.shape[1]
    devices = lax.axis_size("dp")
    half = devices // 2
    piece = width // devices
    group = lax.axis_index("dp")
    core = lax.axis_index("tensor") % 2
    chip_in_group = lax.axis_index("tensor") // 2

    def to_local(a):
        order = [group ^ (2 * high + low) for low in range(2) for high in range(half)]
        return jnp.concatenate([lax.dynamic_slice_in_dim(a, b * piece, piece, 1) for b in order], axis=1)

    def to_true(a):
        order = [group ^ b for b in range(devices)]
        return jnp.concatenate(
            [lax.dynamic_slice_in_dim(a, ((b % 2) * half + b // 2) * piece, piece, 1) for b in order], axis=1
        )

    gains = jnp.stack([attn_gain, ffn_gain])
    gains = jnp.concatenate(
        [gains if low + high == 0 else swap_dp(gains, 2 * high + low) for low in range(2) for high in range(half)], axis=1
    ).astype(F32)
    gain_one, gain_two = gains[0], gains[1]
    gain_query = query_gain.astype(F32)
    gain_key = key_gain.astype(F32)

    qkv_q = gather(jnp.concatenate([w_query, key_matrix, value_matrix], axis=1), 0, True)
    out_q = gather(w_out, 1, False)
    gu_q = gather(jnp.concatenate([w_gate, w_up], axis=1), 0, True)
    down_q = gather(w_down, 1, False)
    qkv_w = [jnp.concatenate(qkv_q[2 * i : 2 * i + 2], axis=0) for i in range(2)]
    out_w = [jnp.concatenate(out_q[2 * i : 2 * i + 2], axis=1) for i in range(2)]
    gu_w = [jnp.concatenate(gu_q[2 * i : 2 * i + 2], axis=0) for i in range(2)]
    down_w = [jnp.concatenate(down_q[2 * i : 2 * i + 2], axis=1) for i in range(2)]

    pair = lax.dynamic_slice(seq_order, (2 * group,), (1,))
    first_len = jnp.sum(jnp.where(jnp.arange(seq_lengths.shape[0], dtype=jnp.int32) == pair[0], seq_lengths, 0))
    row_ids = chip_in_group * chip_rows + jnp.arange(chip_rows, dtype=jnp.int32)
    position = (row_ids - jnp.where(row_ids >= first_len, first_len, 0)).astype(F32)
    freqs = THETA ** (-(jnp.arange(head_size // 2, dtype=F32) * 2.0 / head_size))
    angles = position[:, None] * freqs[None, :]
    cosine = jnp.cos(angles)
    sine = jnp.sin(angles)

    def in_order(own, other):
        return jnp.where(core == 0, jnp.concatenate([own, other], axis=0), jnp.concatenate([other, own], axis=0))

    def own_rows(a):
        return lax.dynamic_slice_in_dim(a, core * rows, rows, 0)

    def other_rows(a):
        return lax.dynamic_slice_in_dim(a, (1 - core) * rows, rows, 0)

    tokens = to_local(tokens)
    cot = to_local(out_grad)
    tokens_full = in_order(tokens, swap_core(tokens)).astype(F32)
    cot_full = jnp.concatenate([cot, swap_core(cot)], axis=0)
    rms_full = lax.rsqrt(jnp.mean(tokens_full * tokens_full, axis=-1, keepdims=True) + EPS)
    normed_one = (tokens_full * rms_full * gain_one).astype(BF16)
    inputs = tokens.astype(F32)
    rms_one = own_rows(rms_full)
    attention, backs = [], []
    for i in range(2):
        projected = dot(normed_one, qkv_w[i])
        query = projected[:, :query_width].reshape(chip_rows, head_count, head_size)
        key_raw = projected[:, query_width : query_width + head_size]
        value_raw = projected[:, query_width + head_size :]
        out, back = attend(query, key_raw, value_raw, gain_query, gain_key, cosine, sine, min(512, chip_rows))
        attention.append(out)
        backs.append(back)

    def pair_dot(a, w, dims=((1,), (0,))):
        return dot(a[0], w[0], dims) + dot(a[1], w[1], dims)

    back_dims = ((1,), (1,))
    att_other = [other_rows(a) for a in attention]
    att_own = [own_rows(a) for a in attention]
    hidden_res = inputs + pair_dot(att_own, out_w) + swap_core(pair_dot(att_other, out_w).astype(BF16)).astype(F32)

    rms_two = lax.rsqrt(jnp.mean(hidden_res * hidden_res, axis=-1, keepdims=True) + EPS)
    normed_two = (hidden_res * rms_two * gain_two).astype(BF16)
    normed_two = jnp.concatenate([normed_two, swap_core(normed_two)], axis=0)
    inner, grad_gu = [], []
    for i in range(2):
        both = dot(normed_two, gu_w[i])
        gate, upper = both[:, :units], both[:, units:]
        sigmoid = jax.nn.sigmoid(gate)
        silu_gate = gate * sigmoid
        inner.append((silu_gate * upper).astype(BF16))
        d_inner = dot(cot_full, down_w[i], back_dims)
        d_silu = sigmoid * (1.0 + gate * (1.0 - sigmoid))
        grad_gu.append(jnp.concatenate([d_inner * upper * d_silu, d_inner * silu_gate], axis=1).astype(BF16))
    down_other = pair_dot([a[rows:] for a in inner], down_w).astype(BF16)
    layer_out = (hidden_res + (pair_dot([a[:rows] for a in inner], down_w) + swap_core(down_other).astype(F32))).astype(BF16)
    layer_out = to_true(layer_out)

    dn_other = pair_dot([a[rows:] for a in grad_gu], gu_w, back_dims).astype(BF16)
    dn_own = pair_dot([a[:rows] for a in grad_gu], gu_w, back_dims) + swap_core(dn_other).astype(F32)
    wide = width // 2
    trans = ((0,), (0,))

    def feature_first(a, b):
        return [dot(a[:, wide * y : wide * (y + 1)], b[x], trans).astype(BF16) for x in range(2) for y in range(2)]

    def feature_last(a, b):
        return [dot(a[x], b[:, wide * y : wide * (y + 1)], trans).astype(BF16) for x in range(2) for y in range(2)]

    d_res, grad_gain_two = norm_back(hidden_res, rms_two, gain_two, dn_own)
    d_res = d_res + cot.astype(F32)
    gu_shard = scatter(feature_first(normed_two, grad_gu), 0, True)
    down_shard = scatter(feature_last(inner, cot_full), 1, False)

    d_res_low = d_res.astype(BF16)
    d_res_full = in_order(d_res_low, swap_core(d_res_low))
    out_shard = scatter(feature_last(attention, d_res_full), 1, False)
    grad_qkv, grad_query_gain, grad_key_gain = [], 0.0, 0.0
    for i in range(2):
        grad, from_query, from_key = backs[i](dot(d_res_full, out_w[i], back_dims).astype(BF16))
        grad_qkv.append(grad)
        grad_query_gain = grad_query_gain + from_query
        grad_key_gain = grad_key_gain + from_key
    da_other = pair_dot([other_rows(a) for a in grad_qkv], qkv_w, back_dims).astype(BF16)
    da_own = pair_dot([own_rows(a) for a in grad_qkv], qkv_w, back_dims) + swap_core(da_other).astype(F32)
    qkv_shard = scatter(feature_first(normed_one, grad_qkv), 0, True)
    d_input, grad_gain_one = norm_back(inputs, rms_one, gain_one, da_own)
    input_grad = to_true((d_input + d_res).astype(BF16))

    head_gains = jnp.concatenate([grad_query_gain, grad_key_gain])[None]
    wide_gains = jnp.stack([grad_gain_one, grad_gain_two])
    for swap in (swap_core, swap_x):
        wide_gains = wide_gains + swap(wide_gains)
        head_gains = head_gains + swap(head_gains)
    step = 1
    while step < devices:
        head_gains = head_gains + swap_dp(head_gains, step)
        step *= 2
    pieces = jnp.split(wide_gains, devices, axis=1)
    own_gains = pieces[0]
    for low in range(2):
        for high in range(half):
            if low + high > 0:
                own_gains = own_gains + swap_dp(pieces[low * half + high], 2 * high + low)
    return (
        layer_out,
        input_grad,
        own_gains[0],
        qkv_shard[:, :query_width],
        qkv_shard[:, query_width : query_width + head_size],
        qkv_shard[:, query_width + head_size :],
        head_gains[0, :head_size],
        head_gains[0, head_size:],
        out_shard,
        own_gains[1],
        gu_shard[:, :units],
        gu_shard[:, units:],
        down_shard,
    )


def solution(mesh):
    placed = (
        P(("dp", "tensor"), None),
        P("dp"),
        P("dp", "tensor"),
        P("dp", "tensor"),
        P("dp", "tensor"),
        P(),
        P(),
        P("tensor", "dp"),
        P("dp"),
        P("dp", "tensor"),
        P("dp", "tensor"),
        P("tensor", "dp"),
        P(("dp", "tensor"), None),
        P(),
        P(),
    )
    return jax.shard_map(
        body,
        mesh=mesh,
        in_specs=placed,
        out_specs=(
            P(("dp", "tensor"), None),
            P(("dp", "tensor"), None),
            P("dp"),
            P("dp", "tensor"),
            P("dp", "tensor"),
            P("dp", "tensor"),
            P(),
            P(),
            P("tensor", "dp"),
            P("dp"),
            P("dp", "tensor"),
            P("dp", "tensor"),
            P("tensor", "dp"),
        ),
        check_vma=False,
    )
```

```python
import jax
import jax.numpy as jnp
from jax import lax
from jax.experimental import pallas as pl
from jax.experimental.pallas import tpu as pltpu
from jax.sharding import PartitionSpec as P


EPS = 1e-06
THETA = 10000.0
F32 = jnp.float32
BF16 = jnp.bfloat16


def swap_core(a):
    return lax.ppermute(a, "tensor", [(t, t ^ 1) for t in range(lax.axis_size("tensor"))])


def swap_x(a):
    return lax.ppermute(a, "tensor", [(t, t ^ 2) for t in range(lax.axis_size("tensor"))])


def swap_dp(a, k):
    return lax.ppermute(a, "dp", [(d, d ^ k) for d in range(lax.axis_size("dp"))])


def halves(a, axis):
    middle = a.shape[axis] // 2
    return lax.slice_in_dim(a, 0, middle, axis=axis), lax.slice_in_dim(a, middle, a.shape[axis], axis=axis)


def gather(block, axis):
    half = lax.axis_size("dp") // 2
    q00 = jnp.concatenate([block] + [swap_dp(block, 2 * k) for k in range(1, half)], axis=axis)
    q01 = swap_dp(q00, 1)
    q10 = swap_x(q00)
    q11 = jnp.concatenate([swap_x(halves(q01, axis)[0]), swap_dp(halves(q10, axis)[1], 1)], axis=axis)
    return q00, q01, q10, q11


def add(*parts):
    total = parts[0].astype(F32)
    for part in parts[1:]:
        total = total + part.astype(F32)
    return total


def scatter(quarters, axis):
    q00, q01, q10, q11 = quarters
    half = lax.axis_size("dp") // 2
    by_x, by_y = halves(q11, axis)
    first, later = halves(q01, axis)
    q01 = jnp.concatenate([add(first, swap_x(by_x)).astype(BF16), later], axis=axis)
    first, later = halves(q10, axis)
    q10 = jnp.concatenate([first, add(later, swap_dp(by_y, 1)).astype(BF16)], axis=axis)
    own = add(q00, swap_dp(q01, 1), swap_x(q10)).astype(BF16)
    blocks = jnp.split(own, half, axis=axis)
    received = [swap_dp(blocks[k], 2 * k) for k in range(1, half)]
    return add(blocks[0], *received)


def norm_back(values, rms, gain, upstream):
    scaled = upstream * gain
    grad_values = rms * scaled - values * (rms * rms * rms) * jnp.mean(
        scaled * values, axis=-1, keepdims=True
    )
    grad_gain = jnp.sum(upstream * values * rms, axis=0)
    return (grad_values, grad_gain)


def dot(a, b, dims=((1,), (0,))):
    return lax.dot_general(a, b, (dims, ((), ())), preferred_element_type=F32)


HEAD = 64
LANES = 2 * HEAD
TILE = 256
LOG2E = 1.4426950408889634


def low_lanes(shape):
    return lax.broadcasted_iota(jnp.int32, shape, 1) < HEAD


def partner(a):
    first = lax.broadcasted_iota(jnp.int32, a.shape, 1) % HEAD < HEAD // 2
    return jnp.where(first, pltpu.roll(a, LANES - HEAD // 2, 1), pltpu.roll(a, HEAD // 2, 1))


def head_mean(a):
    low = low_lanes(a.shape)
    left = jnp.sum(jnp.where(low, a, 0.0), axis=1, keepdims=True)
    right = jnp.sum(jnp.where(low, 0.0, a), axis=1, keepdims=True)
    return jnp.where(low, left, right) * (1.0 / HEAD)


def head_norm(raw, gain, cosine, sine):
    rms = lax.rsqrt(head_mean(raw * raw) + EPS)
    norm = raw * rms * gain
    return rms, norm * cosine + partner(norm) * sine


def head_norm_back(raw, rms, gain, upstream, cosine, sine):
    upstream = upstream * cosine - partner(upstream) * sine
    scaled = upstream * gain
    grad = rms * scaled - raw * (rms * rms * rms) * head_mean(scaled * raw)
    return grad, jnp.sum(upstream * raw * rms, axis=0, keepdims=True)


def both_halves(a, keep_low):
    low = low_lanes(a.shape)
    return jnp.where(low == keep_low, a, pltpu.roll(a, HEAD, 1))


def prepare(proj_ref, gain_ref, cos_ref, sin_ref, q_sc, k_sc, v_sc, kv_t_sc, transposed_low):
    rows = proj_ref.shape[0]
    for start in range(0, rows, TILE):
        at = slice(start, start + TILE)
        cosine, sine = cos_ref[at, :], sin_ref[at, :]
        for pair in range(2):
            raw = proj_ref[at, pair * LANES : (pair + 1) * LANES]
            q_sc[pair, at, :] = head_norm(raw, gain_ref[0:1, :], cosine, sine)[1].astype(BF16)
        raw = proj_ref[at, 2 * LANES : 3 * LANES]
        key = both_halves(head_norm(raw, gain_ref[1:2, :], cosine, sine)[1], True)
        value = both_halves(raw, False)
        k_sc[at, :] = key.astype(BF16)
        v_sc[at, :] = value.astype(BF16)
        kv_t_sc[:, at] = jnp.transpose(key if transposed_low else value).astype(BF16)


def half_of(a, head):
    low = low_lanes(a.shape)
    return jnp.where(low if head == 0 else ~low, a, jnp.zeros_like(a))


def product(a, b, dims=((1,), (0,))):
    return lax.dot_general(a, b, (dims, ((), ())), preferred_element_type=F32)


def causal(a):
    keys = lax.broadcasted_iota(jnp.int32, a.shape, 0)
    return jnp.where(keys <= lax.broadcasted_iota(jnp.int32, a.shape, 1), a, 0.0)


NT = ((1,), (1,))
TO_LOG2 = HEAD ** (-0.5) * LOG2E


def forward_kernel(proj_ref, gain_ref, cos_ref, sin_ref, out_ref, lse_ref, q_sc, k_sc, v_sc, vt_sc):
    rows = proj_ref.shape[0]
    prepare(proj_ref, gain_ref, cos_ref, sin_ref, q_sc, k_sc, v_sc, vt_sc, False)
    for pair in range(2):
        for start in range(0, rows, TILE):
            at = slice(start, start + TILE)
            query = q_sc[pair, at, :]
            halves = []
            for head in range(2):
                q_head = half_of(query, head)
                total = jnp.zeros((1, TILE), F32)
                out = jnp.zeros((HEAD, TILE), F32)
                for key_start in range(0, start + TILE, TILE):
                    keys = slice(key_start, key_start + TILE)
                    expo = jnp.exp2(product(k_sc[keys, :], q_head, NT) * TO_LOG2)
                    if key_start == start:
                        expo = causal(expo)
                    total = total + jnp.sum(expo, axis=0, keepdims=True)
                    out = out + product(vt_sc[:HEAD, keys], expo.astype(BF16))
                halves.append(out / total)
                lse_ref[pair, head : head + 1, at] = jnp.log2(total)
            out_ref[at, pair * LANES : (pair + 1) * LANES] = jnp.transpose(jnp.concatenate(halves, axis=0)).astype(BF16)


def backward_kernel(
    proj_ref, gain_ref, cos_ref, sin_ref, out_ref, lse_ref, up_ref, grad_ref, gain_grad_ref,
    q_sc, k_sc, v_sc, kt_sc, dk_sc, dv_sc,
):
    rows = proj_ref.shape[0]
    scale = HEAD ** (-0.5)
    prepare(proj_ref, gain_ref, cos_ref, sin_ref, q_sc, k_sc, v_sc, kt_sc, True)
    dk_sc[...] = jnp.zeros_like(dk_sc)
    dv_sc[...] = jnp.zeros_like(dv_sc)
    gain_grad = jnp.zeros((1, LANES), F32)
    for pair in range(2):
        lanes = slice(pair * LANES, (pair + 1) * LANES)
        for start in range(0, rows, TILE):
            at = slice(start, start + TILE)
            query = q_sc[pair, at, :]
            up = up_ref[at, lanes]
            weighted = jnp.transpose(up.astype(F32) * out_ref[at, lanes].astype(F32))
            halves = []
            for head in range(2):
                q_head = half_of(query, head)
                up_head = half_of(up, head)
                delta = jnp.sum(weighted[head * HEAD : (head + 1) * HEAD], axis=0, keepdims=True)
                lse = lse_ref[pair, head : head + 1, at]
                grad = jnp.zeros((HEAD, TILE), F32)
                for key_start in range(0, start + TILE, TILE):
                    keys = slice(key_start, key_start + TILE)
                    probs = jnp.exp2(product(k_sc[keys, :], q_head, NT) * TO_LOG2 - lse)
                    if key_start == start:
                        probs = causal(probs)
                    d_probs = product(v_sc[keys, :], up_head, NT)
                    d_scores = (probs * (d_probs - delta)).astype(BF16)
                    dk_sc[keys, :] += product(d_scores, q_head)
                    dv_sc[keys, :] += product(probs.astype(BF16), up_head)
                    grad = grad + product(kt_sc[:HEAD, keys], d_scores)
                halves.append(grad)
            upstream = jnp.transpose(jnp.concatenate(halves, axis=0)) * scale
            raw = proj_ref[at, lanes]
            rms = lax.rsqrt(head_mean(raw * raw) + EPS)
            grad, add_gain = head_norm_back(raw, rms, gain_ref[0:1, :], upstream, cos_ref[at, :], sin_ref[at, :])
            grad_ref[at, lanes] = grad.astype(BF16)
            gain_grad = gain_grad + add_gain
    gain_grad_ref[0:1, :] = gain_grad
    gain_grad = jnp.zeros((1, LANES), F32)
    for start in range(0, rows, TILE):
        at = slice(start, start + TILE)
        raw = proj_ref[at, 2 * LANES : 3 * LANES]
        rms = lax.rsqrt(head_mean(raw * raw) + EPS)
        upstream = dk_sc[at, :]
        upstream = (upstream + pltpu.roll(upstream, HEAD, 1)) * scale
        grad, add_gain = head_norm_back(raw, rms, gain_ref[1:2, :], upstream, cos_ref[at, :], sin_ref[at, :])
        value = dv_sc[at, :]
        value = value + pltpu.roll(value, HEAD, 1)
        grad_ref[at, 2 * LANES : 3 * LANES] = jnp.where(low_lanes(grad.shape), grad, value).astype(BF16)
        gain_grad = gain_grad + add_gain
    gain_grad_ref[1:2, :] = gain_grad


def attend(proj, gains, cosine, sine):
    rows = proj.shape[0]
    return pl.pallas_call(
        forward_kernel,
        name="attend",
        out_shape=(jax.ShapeDtypeStruct((rows, 2 * LANES), BF16), jax.ShapeDtypeStruct((2, 8, rows), F32)),
        scratch_shapes=[
            pltpu.VMEM((2, rows, LANES), BF16),
            pltpu.VMEM((rows, LANES), BF16),
            pltpu.VMEM((rows, LANES), BF16),
            pltpu.VMEM((LANES, rows), BF16),
        ],
    )(proj, gains, cosine, sine)


def attend_back(proj, gains, cosine, sine, out, lse, upstream):
    rows = proj.shape[0]
    return pl.pallas_call(
        backward_kernel,
        name="attend_back",
        out_shape=(jax.ShapeDtypeStruct((rows, 3 * LANES), BF16), jax.ShapeDtypeStruct((2, LANES), F32)),
        scratch_shapes=[
            pltpu.VMEM((2, rows, LANES), BF16),
            pltpu.VMEM((rows, LANES), BF16),
            pltpu.VMEM((rows, LANES), BF16),
            pltpu.VMEM((LANES, rows), BF16),
            pltpu.VMEM((rows, LANES), F32),
            pltpu.VMEM((rows, LANES), F32),
        ],
    )(proj, gains, cosine, sine, out, lse, upstream)


def body(
    tokens,
    attn_gain,
    w_query,
    key_matrix,
    value_matrix,
    query_gain,
    key_gain,
    w_out,
    ffn_gain,
    w_gate,
    w_up,
    w_down,
    out_grad,
    seq_lengths,
    seq_order,
):
    rows, width = tokens.shape
    chip_rows = 2 * rows
    head_size = query_gain.shape[0]
    query_width = w_query.shape[1]
    units = w_gate.shape[1]
    devices = lax.axis_size("dp")
    half = devices // 2
    piece = width // devices
    group = lax.axis_index("dp")
    core = lax.axis_index("tensor") % 2
    chip_in_group = lax.axis_index("tensor") // 2

    def to_local(a):
        order = [group ^ (2 * high + low) for low in range(2) for high in range(half)]
        return jnp.concatenate([lax.dynamic_slice_in_dim(a, b * piece, piece, 1) for b in order], axis=1)

    def to_true(a):
        order = [group ^ b for b in range(devices)]
        return jnp.concatenate(
            [lax.dynamic_slice_in_dim(a, ((b % 2) * half + b // 2) * piece, piece, 1) for b in order], axis=1
        )

    gains = jnp.stack([attn_gain, ffn_gain])
    gains = jnp.concatenate(
        [gains if low + high == 0 else swap_dp(gains, 2 * high + low) for low in range(2) for high in range(half)],
        axis=1,
    ).astype(F32)
    gain_one, gain_two = gains[0], gains[1]
    head_gain = jnp.stack([jnp.tile(query_gain, 2), jnp.tile(key_gain, 2)]).astype(F32)

    qkv_q = gather(jnp.concatenate([w_query, key_matrix, value_matrix], axis=1), 0)
    out_q = gather(w_out, 1)
    gu_q = gather(jnp.concatenate([w_gate, w_up], axis=1), 0)
    down_q = gather(w_down, 1)
    qkv_w = [jnp.concatenate(qkv_q[2 * i : 2 * i + 2], axis=0) for i in range(2)]
    out_w = [jnp.concatenate(out_q[2 * i : 2 * i + 2], axis=1) for i in range(2)]
    gu_w = [jnp.concatenate(gu_q[2 * i : 2 * i + 2], axis=0) for i in range(2)]
    down_w = [jnp.concatenate(down_q[2 * i : 2 * i + 2], axis=1) for i in range(2)]

    pair = lax.dynamic_slice(seq_order, (2 * group,), (1,))
    first_len = jnp.sum(jnp.where(jnp.arange(seq_lengths.shape[0], dtype=jnp.int32) == pair[0], seq_lengths, 0))
    row_ids = chip_in_group * chip_rows + jnp.arange(chip_rows, dtype=jnp.int32)
    position = (row_ids - jnp.where(row_ids >= first_len, first_len, 0)).astype(F32)
    freqs = THETA ** (-(jnp.arange(head_size // 2, dtype=F32) * 2.0 / head_size))
    angles = position[:, None] * freqs[None, :]
    cosine = jnp.cos(angles)
    sine = jnp.sin(angles)
    cosine = jnp.concatenate([cosine] * 4, axis=1)
    sine = jnp.concatenate([-sine, sine, -sine, sine], axis=1)

    def in_order(own, other):
        return jnp.where(core == 0, jnp.concatenate([own, other], axis=0), jnp.concatenate([other, own], axis=0))

    def own_rows(a):
        return lax.dynamic_slice_in_dim(a, core * rows, rows, 0)

    def other_rows(a):
        return lax.dynamic_slice_in_dim(a, (1 - core) * rows, rows, 0)

    tokens = to_local(tokens)
    cot = to_local(out_grad)
    tokens_full = in_order(tokens, swap_core(tokens)).astype(F32)
    cot_full = jnp.concatenate([cot, swap_core(cot)], axis=0)
    square_mean = jnp.mean(tokens_full * tokens_full, axis=-1, keepdims=True)
    rms_full = lax.rsqrt(square_mean + EPS)
    normed_one = (tokens_full * rms_full * gain_one).astype(BF16)
    inputs = tokens.astype(F32)
    rms_one = own_rows(rms_full)
    attention, kept = [], []
    for i in range(2):
        projected = dot(normed_one, qkv_w[i])
        out, lse = attend(projected, head_gain, cosine, sine)
        attention.append(out)
        kept.append((projected, head_gain, cosine, sine, out, lse))

    def pair_dot(a, w, dims=((1,), (0,))):
        first = dot(a[0], w[0], dims)
        return first + dot(a[1], w[1], dims)

    back_dims = ((1,), (1,))
    att_other = [other_rows(a) for a in attention]
    att_own = [own_rows(a) for a in attention]
    branch_other = pair_dot(att_other, out_w).astype(BF16)
    hidden_res = inputs + pair_dot(att_own, out_w) + swap_core(branch_other).astype(F32)

    rms_two = lax.rsqrt(jnp.mean(hidden_res * hidden_res, axis=-1, keepdims=True) + EPS)
    normed_two = (hidden_res * rms_two * gain_two).astype(BF16)
    normed_two = jnp.concatenate([normed_two, swap_core(normed_two)], axis=0)
    inner, grad_gu = [], []
    for i in range(2):
        both = dot(normed_two, gu_w[i])
        gate, upper = both[:, :units], both[:, units:]
        sigmoid = jax.nn.sigmoid(gate)
        silu_gate = gate * sigmoid
        inner.append((silu_gate * upper).astype(BF16))
        d_inner = dot(cot_full, down_w[i], back_dims)
        d_silu = sigmoid * (1.0 + gate * (1.0 - sigmoid))
        grad_gu.append(jnp.concatenate([d_inner * upper * d_silu, d_inner * silu_gate], axis=1).astype(BF16))
    down_other = pair_dot([a[rows:] for a in inner], down_w).astype(BF16)
    layer_out = (hidden_res + (pair_dot([a[:rows] for a in inner], down_w) + swap_core(down_other).astype(F32))).astype(BF16)
    layer_out = to_true(layer_out)

    dn_other = pair_dot([a[rows:] for a in grad_gu], gu_w, back_dims).astype(BF16)
    dn_own = pair_dot([a[:rows] for a in grad_gu], gu_w, back_dims) + swap_core(dn_other).astype(F32)
    wide = width // 2
    trans = ((0,), (0,))

    def weight_grad(a, b, dims):
        return dot(a, b, dims).astype(BF16)

    def feature_first(a, b):
        return [weight_grad(a[:, wide * y : wide * (y + 1)], b[x], trans) for x in range(2) for y in range(2)]

    def feature_last(a, b):
        return [weight_grad(a[x], b[:, wide * y : wide * (y + 1)], trans) for x in range(2) for y in range(2)]

    d_res, grad_gain_two = norm_back(hidden_res, rms_two, gain_two, dn_own)
    d_res = d_res + cot.astype(F32)
    gu_shard = scatter(feature_first(normed_two, grad_gu), 0)
    down_shard = scatter(feature_last(inner, cot_full), 1)

    d_res_low = d_res.astype(BF16)
    d_res_full = in_order(d_res_low, swap_core(d_res_low))
    out_shard = scatter(feature_last(attention, d_res_full), 1)
    grad_qkv, gain_parts = [], []
    for i in range(2):
        upstream = dot(d_res_full, out_w[i], back_dims).astype(BF16)
        grad, part = attend_back(*kept[i], upstream)
        grad_qkv.append(grad)
        gain_parts.append(part)
    gain_parts = gain_parts[0] + gain_parts[1]
    da_other = pair_dot([other_rows(a) for a in grad_qkv], qkv_w, back_dims).astype(BF16)
    da_own = pair_dot([own_rows(a) for a in grad_qkv], qkv_w, back_dims) + swap_core(da_other).astype(F32)
    qkv_shard = scatter(feature_first(normed_one, grad_qkv), 0)
    d_input, grad_gain_one = norm_back(inputs, rms_one, gain_one, da_own)
    input_grad = to_true((d_input + d_res).astype(BF16))

    head_gains = gain_parts[0:1, :head_size] + gain_parts[0:1, head_size:]
    head_gains = jnp.concatenate([head_gains, gain_parts[1:2, :head_size]], axis=1)
    head_gains = head_gains.reshape(2, head_size)
    wide_gains = jnp.concatenate([jnp.stack([grad_gain_one, grad_gain_two]), head_gains], axis=1)
    wide_gains = wide_gains + swap_core(wide_gains)
    wide_gains = wide_gains + swap_x(wide_gains)
    head_gains = wide_gains[:, width:]
    own_gains = jnp.concatenate([wide_gains[:, :piece], head_gains], axis=1)
    for low in range(2):
        for high in range(half):
            if low + high > 0:
                start = (low * half + high) * piece
                part = jnp.concatenate([wide_gains[:, start : start + piece], head_gains], axis=1)
                own_gains = own_gains + swap_dp(part, 2 * high + low)
    return (
        layer_out,
        input_grad,
        own_gains[0, :piece],
        qkv_shard[:, :query_width],
        qkv_shard[:, query_width : query_width + head_size],
        qkv_shard[:, query_width + head_size :],
        own_gains[0, piece:],
        own_gains[1, piece:],
        out_shard,
        own_gains[1, :piece],
        gu_shard[:, :units],
        gu_shard[:, units:],
        down_shard,
    )


def solution(mesh):
    placed = (
        P(("dp", "tensor"), None),
        P("dp"),
        P("dp", "tensor"),
        P("dp", "tensor"),
        P("dp", "tensor"),
        P(),
        P(),
        P("tensor", "dp"),
        P("dp"),
        P("dp", "tensor"),
        P("dp", "tensor"),
        P("tensor", "dp"),
        P(("dp", "tensor"), None),
        P(),
        P(),
    )
    return jax.shard_map(
        body,
        mesh=mesh,
        in_specs=placed,
        out_specs=(
            P(("dp", "tensor"), None),
            P(("dp", "tensor"), None),
            P("dp"),
            P("dp", "tensor"),
            P("dp", "tensor"),
            P("dp", "tensor"),
            P(),
            P(),
            P("tensor", "dp"),
            P("dp"),
            P("dp", "tensor"),
            P("dp", "tensor"),
            P("tensor", "dp"),
        ),
        check_vma=False,
    )
```
